32 devices in a mesh: kt: 4 (over z), ks: 8 (over y, x, core).
Axes of the slice: x: 2, y: 2, z: 4, core: 2. Of those that a mesh axis runs over, the one named last changes fastest.
Arguments:
- val_target: bfloat16 [8, 32, 512], P('kt', None, 'ks'), may hold values from -6 to 6
- cond_target: bfloat16 [8, 64, 512], P('kt', None, 'ks'), may hold values from -0.046875 to 0.046875
- val_source: bfloat16 [32, 32, 512], P('ks', None, 'kt'), may hold values from -6 to 6
- cond_source: bfloat16 [32, 64, 512], P('ks', None, 'kt'), may hold values from -0.125 to 0.125
- trial_vectors: bfloat16 [32, 16, 2048], P('ks', 'kt'), may hold values from -6 to 6
- screened: bfloat16 [512, 512, 512], P(None, ('kt', 'ks')), may hold values from -0.25 to 0.25
- pair_momentum: int32 [8, 32], replicated, may hold values from 0 to 511
Outputs:
- kernel_out: float32 [8, 16, 2048], P('kt', 'ks')
The draws below stay inside these ranges and needn't reach their ends.
All inputs are finite; a program needn't handle non-finite values.
Results may differ from the reference program's by a relative error of at most 0.019.
Values may be sent and summed in bfloat16 or wider, within the bound.
A program may use at most 128 MiB of HBM per device.

```python
import jax
import jax.numpy as jnp
from jax import lax

NAUX = 512
NV = 32
NC = 64
NVEC = 16
NQ = 512
NKT = 8
NKS = 32


def plant(drawn, own_key, low, top_value):
    spot = [jax.random.randint(jax.random.fold_in(own_key, axis), (), 0, length) for axis, length in enumerate(drawn.shape)]
    longest = drawn.shape.index(max(drawn.shape))
    next_to = spot[:longest] + [(spot[longest] + 1) % drawn.shape[longest]] + spot[longest + 1:]
    return drawn.at[tuple(spot)].set(low).at[tuple(next_to)].set(top_value)


def block_levels(rng, shape, cuts, least, high):
    def one(axis_at, parts):
        heights = jax.random.uniform(jax.random.fold_in(jax.random.fold_in(rng, 6), axis_at), (parts,), jnp.float32, least / len(cuts), high / len(cuts))
        return jnp.repeat(jnp.exp(heights), shape[axis_at] // parts).reshape((-1,) + (1,) * (len(shape) - axis_at - 1))

    gain = one(*cuts[0])
    for cut in cuts[1:]:
        gain = gain * one(*cut)
    return gain


def bell_draw(rng, extent, width, reach, pieces=(), kind=jnp.bfloat16):
    factor_of = block_levels(rng, extent, pieces, -0.22, 0.18) if pieces else 1.0
    drawn = jax.random.normal(rng, extent, jnp.float32) * width * factor_of
    return jnp.minimum(jnp.maximum(drawn, -reach), reach).astype(kind)


def setup_inputs(seed: int = 0) -> dict:
    key_list = jax.random.split(jax.random.key(seed), 8)
    return {
        "val_target": bell_draw(key_list[0], (NKT, NV, NAUX), 1.0, 6.0, ((0, 4), (2, 8))),
        "cond_target": bell_draw(key_list[1], (NKT, NC, NAUX), (NAUX * NKS) ** -0.5, 0.046875, ((0, 4), (2, 8))),
        "val_source": bell_draw(key_list[2], (NKS, NV, NAUX), 1.0, 6.0, ((0, 8), (2, 4))),
        "cond_source": bell_draw(key_list[3], (NKS, NC, NAUX), (NC * NV) ** -0.5, 0.125, ((0, 8), (2, 4))),
        "trial_vectors": bell_draw(key_list[4], (NKS, NVEC, NV * NC), 1.0, 6.0, ((0, 8), (1, 4))),
        "screened": bell_draw(key_list[5], (NQ, NAUX, NAUX), NAUX ** -0.5, 0.25, ((1, 32),)),
        "pair_momentum": plant(jax.random.randint(key_list[6], (NKT, NKS), 0, NQ), jax.random.fold_in(key_list[6], 1), 0, NQ - 1).astype(jnp.int32),
    }


def reference(val_target, cond_target, val_source, cond_source, trial_vectors, screened, pair_momentum):
    highest = lax.Precision.HIGHEST
    trial_four = trial_vectors.reshape(NKS, NVEC, NV, NC).astype(jnp.float32)
    dressed = jnp.einsum("snwc,scq->snwq", trial_four, cond_source.astype(jnp.float32), precision=highest)
    dressed = dressed.astype(jnp.bfloat16).astype(jnp.float32)

    def one_target(index):
        momentum = pair_momentum[index]
        kernel_mats = screened[momentum].astype(jnp.float32)
        target_val = val_target[index].astype(jnp.float32)
        pair_prod = (target_val[None, :, None, :] * val_source.astype(jnp.float32)[:, None, :, :]).astype(jnp.bfloat16)
        kernels = jnp.einsum("svwp,spq->svwq", pair_prod.astype(jnp.float32), kernel_mats, precision=highest)
        kernels = kernels.astype(jnp.bfloat16).astype(jnp.float32)
        reduced = jnp.einsum("svwq,snwq->vnq", kernels, dressed, precision=highest)
        reduced = reduced.astype(jnp.bfloat16).astype(jnp.float32)
        result = jnp.einsum("vnq,cq->nvc", reduced, cond_target[index].astype(jnp.float32), precision=highest)
        return result.reshape(NVEC, NV * NC)

    return lax.map(one_target, jnp.arange(NKT, dtype=jnp.int32))
```

```python
import functools

import jax
import jax.numpy as jnp
from jax import lax
from jax.experimental import pallas as pl
from jax.experimental.pallas import tpu as pltpu
from jax.sharding import PartitionSpec as P


def general(val_target, cond_target, val_source, cond_source, trial_vectors, screened, pair_momentum):
    tgt_val, tgt_cond = (
        lax.all_gather(val_target, "ks", axis=2, tiled=True),
        lax.all_gather(cond_target, "ks", axis=2, tiled=True),
    )
    src_val, src_cond, vectors = (
        lax.all_gather(val_source, "kt", axis=2, tiled=True),
        lax.all_gather(cond_source, "kt", axis=2, tiled=True),
        lax.all_gather(trial_vectors, "kt", axis=1, tiled=True),
    )
    count_kt = lax.axis_size("kt")
    count_ks = lax.axis_size("ks")
    tgt_count = tgt_val.shape[0]
    src_count = src_val.shape[0]
    pair_count = tgt_count * src_count
    width = screened.shape[2]
    val_bands = tgt_val.shape[1]
    cond_bands = tgt_cond.shape[1]
    vec_count = vectors.shape[1]
    table = pair_momentum.reshape(count_kt, tgt_count, count_ks, src_count)
    table = table.transpose(1, 3, 0, 2).reshape(pair_count, count_kt * count_ks)
    outgoing = screened[table]
    arrived = lax.all_to_all(outgoing, ("kt", "ks"), split_axis=1, concat_axis=1, tiled=True)
    pair_mats = arrived.reshape(tgt_count, src_count, width, width)
    trial_four = vectors.reshape(src_count, vec_count, val_bands, cond_bands)
    dressed = jnp.einsum(
        "snwc,scq->snwq", trial_four, src_cond, preferred_element_type=jnp.float32
    ).astype(jnp.bfloat16)
    pair_prod = (
        tgt_val.astype(jnp.float32)[:, None, :, None, :]
        * src_val.astype(jnp.float32)[None, :, None, :, :]
    ).astype(jnp.bfloat16)
    kernels = jnp.einsum(
        "tsvwp,tspq->tsvwq", pair_prod, pair_mats, preferred_element_type=jnp.float32
    ).astype(jnp.bfloat16)
    reduced = jnp.einsum(
        "tsvwq,snwq->tvnq", kernels, dressed, preferred_element_type=jnp.float32
    ).astype(jnp.bfloat16)
    partial_out = jnp.einsum(
        "tvnq,tcq->tnvc", reduced, tgt_cond, preferred_element_type=jnp.float32
    )
    partial_out = partial_out.reshape(tgt_count, vec_count, val_bands * cond_bands)
    return lax.psum_scatter(
        partial_out.astype(jnp.bfloat16), "ks", scatter_dimension=1, tiled=True
    ).astype(jnp.float32)


MESH = pl.DeviceIdType.MESH
VMEM = pl.BlockSpec(memory_space=pltpu.VMEM)


def remote(src, dst, send, recv, kt, ks):
    return pltpu.make_async_remote_copy(
        src_ref=src, dst_ref=dst, send_sem=send, recv_sem=recv, device_id=(kt, ks), device_id_type=MESH
    )


def fused_kernel(nz, ns, nt, nsl, table, screened, block, vsx, vtx, result,
                 out, vsg, vtg, slab, wide, mbuf, abuf, sent, got,
                 zs, zr, xs, xr, ys, yr, as_, ar, bs, br, ps, pr, vss, vsr, vts, vtr, fs, fr, ls):
    z, k = lax.axis_index("kt"), lax.axis_index("ks")
    core = lax.rem(k, 2)
    side = lax.rem(k // 2, 2)
    kx = k + 2 - 4 * side
    ky = lax.rem(k + 4, ns)
    kd = lax.rem(kx + 4, ns)
    kp = k + 1 - 2 * core
    other = [kp, kx + 1 - 2 * core, lax.rem(kp + 4, ns), lax.rem(kx + 5 - 2 * core, ns)]
    half = block.shape[0] // 2
    first, second = pl.ds(0, half), pl.ds(half, half)
    zpeer = [lax.rem(z + j, nz) for j in range(nz)]
    speer = [lax.rem(k + j, ns) for j in range(ns)]
    me = z * ns + k
    count = nz * ns

    load = pltpu.make_async_copy(screened, slab, ls.at[3])
    load.start()
    own = [
        pltpu.make_async_copy(block, out.at[me], ls.at[0]),
        pltpu.make_async_copy(vsx.at[k], vsg.at[k], ls.at[1]),
        pltpu.make_async_copy(vtx, vtg.at[k], ls.at[2]),
    ]
    for copy in own:
        copy.start()

    barrier = pltpu.get_barrier_semaphore()

    def hello(j, carry):
        peer = lax.rem(me + j, count)
        pl.semaphore_signal(barrier, inc=1, device_id=(peer // ns, lax.rem(peer, ns)), device_id_type=MESH)
        return carry

    lax.fori_loop(1, count, hello, 0)
    pl.semaphore_wait(barrier, count - 1)

    slot = lambda zz, kk: out.at[zz * ns + kk]
    started = []

    def go(copy):
        copy.start()
        started.append(copy)

    def arrived(dst, recv):
        remote(dst, dst, recv, recv, z, kp).wait_recv()

    def partner(index, src, zz, kk):
        go(remote(src, slot(zz, kk), ps.at[index], pr.at[index], z, kp))

    for j in range(1, ns):
        go(remote(vsx.at[speer[j]], vsg.at[k], vss.at[j], vsr.at[j], z, speer[j]))
    for j in (1, nz - 1, *range(2, nz - 1)):
        go(remote(block, slot(z, k), zs.at[j], zr.at[nz - j], zpeer[j], k))
    go(remote(block, slot(z, k), xs.at[0], xr.at[0], z, kx))
    go(remote(block, slot(z, k), ys.at[0], yr.at[0], z, ky))
    partner(0, block, z, k)
    for j in range(1, ns):
        go(remote(vtx, vtg.at[k], vts.at[j], vtr.at[j], z, speer[j]))

    order = [0, 1, nz - 1, *range(2, nz - 1)]

    def spread(j):
        zz = zpeer[j]
        arrived(slot(zz, k), zr.at[j])
        go(remote(slot(zz, k), slot(zz, k), xs.at[j], xr.at[j], z, kx))
        go(remote(slot(zz, k), slot(zz, k), ys.at[j], yr.at[j], z, ky))
        partner(j, slot(zz, k), zz, k)

    def relay(j):
        zz = zpeer[j]
        arrived(slot(zz, kx), xr.at[j])
        go(remote(slot(zz, kx).at[first], slot(zz, kx).at[first], as_.at[j], ar.at[j], z, ky))
        partner(nz + j, slot(zz, kx), zz, kx)
        arrived(slot(zz, ky), yr.at[j])
        go(remote(slot(zz, ky).at[second], slot(zz, ky).at[second], bs.at[j], br.at[j], z, kx))
        partner(2 * nz + j, slot(zz, ky), zz, ky)

    def corner(j):
        zz = zpeer[j]
        arrived(slot(zz, kd).at[first], ar.at[j])
        arrived(slot(zz, kd).at[second], br.at[j])
        partner(3 * nz + j, slot(zz, kd), zz, kd)

    def passed(piece):
        for j in range(nz):
            arrived(slot(zpeer[j], other[piece]), pr.at[piece * nz + j])

    rows, width = slab.shape[1:]
    tgt = nz * nt
    nvec = mbuf.shape[2]
    lanes = 128
    halves = nvec // nz // 2
    depth = vsg.shape[2] // nsl
    shape = (nsl * rows, nsl * depth)
    picked = lax.broadcasted_iota(jnp.int32, shape, 0) // rows == lax.broadcasted_iota(jnp.int32, shape, 1) // depth
    trial_rows = halves * nsl * depth
    cond = lanes // 2
    group = 4
    qblocks = width // lanes

    def compute(b, fresh=False):
        low = lax.broadcasted_iota(jnp.int32, (rows, lanes), 1) < lanes // 2
        left = jnp.concatenate([vsg[b].astype(jnp.float32)] * nsl, axis=0)
        left = jnp.where(picked, left, 0.0).astype(jnp.bfloat16)
        right = jnp.concatenate(
            [out[zz * ns + b, h * nsl * depth:(h + 1) * nsl * depth, :] for zz in range(nz) for h in range(halves)],
            axis=1,
        )
        folded = jnp.dot(left, right, preferred_element_type=jnp.float32)
        for s in range(nsl):
            parts = []
            for j in range(nvec // 2):
                piece = folded[s * rows:(s + 1) * rows, j * lanes:(j + 1) * lanes]
                parts += [jnp.where(low, piece, 0.0), jnp.where(low, 0.0, piece)]
            left_s = jnp.concatenate(parts, axis=0).astype(jnp.bfloat16)
            at = trial_rows + s * cond
            cond_s = jnp.concatenate([out[zz * ns + b, at:at + cond, :] for zz in range(nz)], axis=1)
            right_s = jnp.concatenate([cond_s, cond_s], axis=0)
            full = jnp.dot(left_s, right_s, preferred_element_type=jnp.float32).astype(jnp.bfloat16)
            for q in range(qblocks):
                mbuf[q, s] = full[:, q * lanes:(q + 1) * lanes].reshape(nvec, rows, lanes)

        def widen(t, carry):
            for s in range(nsl):
                w = slab[table[t, b * nsl + s]]
                for q in range(qblocks):
                    wide[q, t * nsl + s] = w[:, q * lanes:(q + 1) * lanes]
            return carry

        lax.fori_loop(0, tgt, widen, 0)

        def tile(q, carry):
            for t0 in range(0, tgt, group):
                w = [[wide[q, (t0 + t) * nsl + s] for s in range(nsl)] for t in range(group)]
                for n in range(nvec):
                    m = [mbuf[q, s, n] for s in range(nsl)]
                    for t in range(group):
                        terms = [w[t][s] * m[s] for s in range(nsl)]
                        while len(terms) > 1:
                            terms = [sum(terms[i:i + 2][1:], terms[i]) for i in range(0, len(terms), 2)]
                        value = terms[0] if fresh else abuf[q, t0 + t, n] + terms[0]
                        abuf[q, t0 + t, n] = value
            return carry

        lax.fori_loop(0, qblocks, tile, 0)

    spread(order[1])
    relay(order[0])
    spread(order[2])
    relay(order[1])
    corner(order[0])
    for j in order[3:]:
        spread(j)
    for copy in own:
        copy.wait()
    for j in range(1, ns):
        arrived(vsg.at[speer[ns - j]], vsr.at[j])
    load.wait()
    compute(k, True)
    passed(0)
    compute(kp)
    relay(order[2])
    corner(order[1])
    for place in range(3, nz):
        relay(order[place])
    compute(kx)
    for place in range(2, nz - 1):
        corner(order[place])
    compute(ky)
    corner(order[-1])
    passed(1)
    passed(2)

    def later(i, carry):
        one = i // 2
        sx = lax.rem(i + 1, 2) * one + (1 - one) * lax.rem(i, 2)
        sy = (1 - one) + one * lax.rem(i, 2)
        kc = k + one * (1 - 2 * core)
        compute(lax.rem(kc + sx * (2 - 4 * side) + 4 * sy, ns))
        return carry

    lax.fori_loop(1, 4, later, 0)
    passed(3)
    compute(other[3])

    lowc = lax.broadcasted_iota(jnp.int32, (nvec * rows, lanes), 1) < lanes // 2
    at = trial_rows + nsl * cond
    chunk = sent.shape[1] // ns

    def deal(dz, dk):
        zz, kk = lax.rem(z + dz, nz), lax.rem(k + dk, ns)
        src = sent.at[zz, pl.ds(pl.multiple_of(kk * chunk, chunk), chunk)]
        return remote(src, got.at[me], fs.at[dz, dk], fr.at[dz, dk], zz, kk)

    def emit(i, carry):
        dz = lax.rem(i + 1, nz)
        zz = lax.rem(z + dz, nz)
        right = jnp.concatenate([out[zz * ns + b, at:, :] for b in range(ns)], axis=0)
        pair = []
        for t in range(nt):
            parts = [abuf[q, zz * nt + t].reshape(nvec * rows, lanes) for q in range(qblocks)]
            pair.append(jnp.dot(jnp.concatenate(parts, axis=1), right, preferred_element_type=jnp.float32))
        sent[zz] = jnp.where(lowc, pair[0], pair[1]).astype(jnp.bfloat16)

        def push(dk, carry):
            deal(dz, dk).start()
            return carry

        lax.fori_loop((i + 1) // nz, ns, push, 0)
        return carry

    lax.fori_loop(0, nz, emit, 0)
    mine = pltpu.make_async_copy(sent.at[z, pl.ds(pl.multiple_of(k * chunk, chunk), chunk)], got.at[me], ls.at[4])
    mine.start()
    mine.wait()
    for copy in started:
        copy.wait_send()
    for j in range(1, ns):
        arrived(vtg.at[speer[ns - j]], vtr.at[j])

    def settle(i, carry):
        dz, dk = i // ns, lax.rem(i, ns)
        deal(dz, dk).wait_send()
        giver = got.at[lax.rem(z + nz - dz, nz) * ns + lax.rem(k + ns - dk, ns)]
        remote(giver, giver, fs.at[dz, dk], fr.at[dz, dk], z, kp).wait_recv()
        return carry

    lax.fori_loop(1, count, settle, 0)
    left = jnp.concatenate([vtg[b] for b in range(ns)], axis=1)
    for n in range(result.shape[0]):
        right = jnp.concatenate([got[i, n * rows:(n + 1) * rows, :] for i in range(count)], axis=0)
        result[n] = jnp.dot(left, right, preferred_element_type=jnp.float32)


def local(val_target, cond_target, val_source, cond_source, trial_vectors, screened, pair_momentum):
    nz, ns = lax.axis_size("kt"), lax.axis_size("ks")
    nt, bands, pk = val_target.shape
    nc = cond_target.shape[1]
    nsl, _, pz = val_source.shape
    nv = trial_vectors.shape[1]
    rows, width = screened.shape[1:]
    nvec = nv * nz
    nloc = nvec // ns
    bf16, f32 = jnp.bfloat16, jnp.float32
    trial = trial_vectors.reshape(nsl, nv // 2, 2, bands, nc).transpose(1, 0, 3, 2, 4).reshape(-1, 2 * nc)
    block = jnp.concatenate(
        [trial, cond_source.reshape(nsl * nc, pz), cond_target.transpose(2, 0, 1).reshape(pk, nt * nc)], axis=0
    )
    vsx = val_source.reshape(nsl, bands, ns, rows).transpose(2, 3, 0, 1).reshape(ns, rows, nsl * bands)
    vtx = val_target.reshape(nt * bands, pk)
    dma = pltpu.SemaphoreType.DMA
    wide = pl.pallas_call(
        functools.partial(fused_kernel, nz, ns, nt, nsl),
        out_shape=jax.ShapeDtypeStruct((nloc, nt * bands, nt * nc), f32),
        in_specs=[pl.BlockSpec(memory_space=pltpu.SMEM), pl.BlockSpec(memory_space=pl.ANY)] + [VMEM] * 3,
        out_specs=VMEM,
        scratch_shapes=[
            pltpu.VMEM((nz * ns, *block.shape), bf16),
            pltpu.VMEM(vsx.shape, bf16),
            pltpu.VMEM((ns, *vtx.shape), bf16),
            pltpu.VMEM(screened.shape, bf16),
            pltpu.VMEM((width // 128, nz * nt * nsl, rows, 128), bf16),
            pltpu.VMEM((width // 128, nsl, nvec, rows, 128), bf16),
            pltpu.VMEM((width // 128, nz * nt, nvec, rows, 128), bf16),
            pltpu.VMEM((nz, nvec * rows, nt * nc), bf16),
            pltpu.VMEM((nz * ns, nloc * rows, nt * nc), bf16),
        ]
        + [dma((nz,))] * 10 + [dma((4 * nz,))] * 2 + [dma((ns,))] * 4 + [dma((nz, ns))] * 2 + [dma((5,))],
        compiler_params=pltpu.CompilerParams(
            collective_id=0, has_side_effects=True, vmem_limit_bytes=48 * 2**20
        ),
        name="fused",
    )(pair_momentum, screened, block, vsx, vtx)
    wide = wide.reshape(nloc, nt, bands, nt, nc)
    result = jnp.stack([wide[:, t, :, t, :] for t in range(nt)], axis=0)
    return result.reshape(nt, nloc, bands * nc)


def fits(mesh, args):
    val_target, cond_target, val_source, cond_source, trial_vectors, screened, pair_momentum = args
    nz, ns = mesh.shape["kt"], mesh.shape["ks"]
    aux = val_target.shape[2]
    nt, nvec, nc = val_target.shape[0] // nz, trial_vectors.shape[1], cond_target.shape[1]
    rows = aux // (nz * ns)
    return (
        ns == 8 and nz >= 4 and nt == 2 and 2 * nc == 128 and aux // nz == 128 and rows == 16
        and nvec % (2 * nz) == 0 and nvec % ns == 0 and pair_momentum.size <= 256
    )


def solution(mesh):
    in_specs = (
        P("kt", None, "ks"),
        P("kt", None, "ks"),
        P("ks", None, "kt"),
        P("ks", None, "kt"),
        P("ks", "kt", None),
        P(None, ("kt", "ks"), None),
        P(),
    )
    out_specs = P("kt", "ks", None)

    def whole(*args):
        body = local if fits(mesh, args) else general
        return jax.shard_map(body, mesh=mesh, in_specs=in_specs, out_specs=out_specs, check_vma=False)(*args)

    return whole
```

```python
import functools

import jax
import jax.numpy as jnp
from jax import lax
from jax.experimental import pallas as pl
from jax.experimental.pallas import tpu as pltpu
from jax.sharding import PartitionSpec as P


def general(val_target, cond_target, val_source, cond_source, trial_vectors, screened, pair_momentum):
    tgt_val, tgt_cond = (
        lax.all_gather(val_target, "ks", axis=2, tiled=True),
        lax.all_gather(cond_target, "ks", axis=2, tiled=True),
    )
    src_val, src_cond, vectors = (
        lax.all_gather(val_source, "kt", axis=2, tiled=True),
        lax.all_gather(cond_source, "kt", axis=2, tiled=True),
        lax.all_gather(trial_vectors, "kt", axis=1, tiled=True),
    )
    count_kt = lax.axis_size("kt")
    count_ks = lax.axis_size("ks")
    tgt_count = tgt_val.shape[0]
    src_count = src_val.shape[0]
    pair_count = tgt_count * src_count
    width = screened.shape[2]
    val_bands = tgt_val.shape[1]
    cond_bands = tgt_cond.shape[1]
    vec_count = vectors.shape[1]
    table = pair_momentum.reshape(count_kt, tgt_count, count_ks, src_count)
    table = table.transpose(1, 3, 0, 2).reshape(pair_count, count_kt * count_ks)
    outgoing = screened[table]
    arrived = lax.all_to_all(outgoing, ("kt", "ks"), split_axis=1, concat_axis=1, tiled=True)
    pair_mats = arrived.reshape(tgt_count, src_count, width, width)
    trial_four = vectors.reshape(src_count, vec_count, val_bands, cond_bands)
    dressed = jnp.einsum(
        "snwc,scq->snwq", trial_four, src_cond, preferred_element_type=jnp.float32
    ).astype(jnp.bfloat16)
    pair_prod = (
        tgt_val.astype(jnp.float32)[:, None, :, None, :]
        * src_val.astype(jnp.float32)[None, :, None, :, :]
    ).astype(jnp.bfloat16)
    kernels = jnp.einsum(
        "tsvwp,tspq->tsvwq", pair_prod, pair_mats, preferred_element_type=jnp.float32
    ).astype(jnp.bfloat16)
    reduced = jnp.einsum(
        "tsvwq,snwq->tvnq", kernels, dressed, preferred_element_type=jnp.float32
    ).astype(jnp.bfloat16)
    partial_out = jnp.einsum(
        "tvnq,tcq->tnvc", reduced, tgt_cond, preferred_element_type=jnp.float32
    )
    partial_out = partial_out.reshape(tgt_count, vec_count, val_bands * cond_bands)
    return lax.psum_scatter(
        partial_out.astype(jnp.bfloat16), "ks", scatter_dimension=1, tiled=True
    ).astype(jnp.float32)


MESH = pl.DeviceIdType.MESH
HBM = pl.BlockSpec(memory_space=pltpu.MemorySpace.HBM)
C, X = range(2)
UP, DOWN, ACROSS_X, ACROSS_Y, HALF_Y, HALF_X, PARTNER = range(7)
LANES = 128


def remote(src, dst, send, recv, kt, ks):
    return pltpu.make_async_remote_copy(
        src_ref=src, dst_ref=dst, send_sem=send, recv_sem=recv, device_id=(kt, ks), device_id_type=MESH
    )


def nearest(nz):
    packed = []
    for place in range(nz):
        word = 0
        for own in range(nz):
            ranked = sorted(range(nz), key=lambda other: (abs(other - own), other))
            word |= ranked[place] << (2 * own)
        packed.append(word)
    return packed


def one_hot(shape, hit):
    row = lax.broadcasted_iota(jnp.int32, shape, 0)
    col = lax.broadcasted_iota(jnp.int32, shape, 1)
    return jnp.where(hit(row, col), 1.0, 0.0).astype(jnp.bfloat16)


def dot(a, b):
    return jnp.dot(a, b, preferred_element_type=jnp.float32)


def dot_t(a, b):
    return lax.dot_general(a, b, (((1,), (1,)), ((), ())), preferred_element_type=jnp.float32)


def fused_kernel(wbuf, mbuf, abuf, fbuf, nz, ns, table_in, screened, vt_in, ct_in, vs_in, cs_in, tr_in, result,
                 cb, xb, vsg, vtg, slab, trv, vsv, ctv, table, sent, got,
                 ss, rs, vss, vsr, vts, vtr, fs, fr, ls):
    bf16, f32 = jnp.bfloat16, jnp.float32
    z, k = lax.axis_index("kt"), lax.axis_index("ks")
    core, side, deep = lax.rem(k, 2), lax.rem(k // 2, 2), k // 4

    def flipped(c):
        return lax.rem(core + c % 2, 2) + 2 * lax.rem(side + (c // 2) % 2, 2) + 4 * lax.rem(deep + c // 4, 2)

    kk = [flipped(c) for c in range(ns)]
    kp, kx, ky, kd = kk[1], kk[2], kk[4], kk[6]
    me = z * ns + k
    z_up, z_down = z + 1, z - 1
    near = [lax.rem(lax.shift_right_logical(jnp.int32(word), 2 * z), 4) for word in nearest(nz)]
    bufs = [cb, xb]
    nsl, bands, depth = vs_in.shape
    nt, _, pk = vt_in.shape
    nc = ct_in.shape[1]
    nv = tr_in.shape[1]
    rows, width = slab.shape[1:]
    nsrc, tgt, nvec = ns * nsl, nz * nt, nz * nv
    half_w = bands // 2
    near_word = sum(near[j] * 4 ** j for j in range(nz))

    local = [
        (tr_in, trv), (vs_in, vsv), (ct_in, ctv), (cs_in, cb.at[me, pl.ds(0, nsl * nc)]), (vt_in, vtg.at[k]), (table_in, table), (screened, slab),
    ]
    local = [pltpu.make_async_copy(src, dst, ls.at[i]) for i, (src, dst) in enumerate(local)]
    for copy in local:
        copy.start()

    barrier = pltpu.get_barrier_semaphore()

    def greet(kt, ks):
        pl.semaphore_signal(barrier, inc=1, device_id=(kt, ks), device_id_type=MESH)

    has_up, has_down = z < nz - 1, z > 0
    for peer in (kp, kx, ky):
        greet(z, peer)
    pl.when(has_up)(lambda: greet(z + 1, k))
    pl.when(has_down)(lambda: greet(z - 1, k))

    local[2].wait()
    cb[me, nsl * nc:] = dot_t(one_hot((pk, pk), lambda r, c: r == c), ctv[...].reshape(nt * nc, pk)).astype(bf16)
    inner = jnp.logical_and(has_up, has_down)
    pl.when(inner)(lambda: pl.semaphore_wait(barrier, 5))
    pl.when(jnp.logical_not(inner))(lambda: pl.semaphore_wait(barrier, 4))

    started, guard = [], []

    def go(make, when=None):
        conds = guard + ([] if when is None else [when])
        started.append((make, conds))
        if when is None:
            make().start()
        else:
            pl.when(when)(lambda: make().start())

    def under(cond, body):
        guard.append(cond)
        pl.when(cond)(body)
        guard.pop()

    def both(d, body):
        if d == 0:
            body(z, None)
        else:
            for zz, there, below in ((z - d, z >= d, True), (z + d, z + d < nz, False)):
                under(there, functools.partial(body, zz, below))

    def slot(ty, zz, col):
        return bufs[ty].at[zz * ns + col]

    def part(ty, zz, col, second):
        n = bufs[ty].shape[1] // 2
        return slot(ty, zz, col).at[pl.ds(n * second, n)]

    def send(kind, ty, zz, col, kt, ks, when=None, src=None, second=None):
        def make():
            dst = slot(ty, zz, col) if second is None else part(ty, zz, col, second)
            return remote(dst if src is None else src, dst, ss.at[kind, ty, zz], rs.at[kind, ty, zz], kt, ks)

        go(make, when)

    def landed(kind, ty, zz, col, second=None):
        dst = slot(ty, zz, col) if second is None else part(ty, zz, col, second)
        remote(dst, dst, ss.at[kind, ty, zz], rs.at[kind, ty, zz], z, kp).wait_recv()

    def launch_z(ty, src=None):
        send(UP, ty, z, k, z_up, k, has_up, src)
        send(DOWN, ty, z, k, z_down, k, has_down, src)

    def launch_xy(ty):
        send(ACROSS_X, ty, z, k, z, kx)
        send(ACROSS_Y, ty, z, k, z, ky)
        send(PARTNER, ty, z, k, z, kp)

    def own(ty, d):
        def body(zz, below):
            landed(UP if below else DOWN, ty, zz, k)
            if below:
                send(UP, ty, zz, k, z_up, k, has_up)
            else:
                send(DOWN, ty, zz, k, z_down, k, has_down)
            send(ACROSS_X, ty, zz, k, z, kx)
            send(ACROSS_Y, ty, zz, k, z, ky)
            send(PARTNER, ty, zz, k, z, kp)

        both(d, body)

    def side_columns(ty, d):
        def body(zz, below):
            landed(ACROSS_X, ty, zz, kx)
            send(HALF_Y, ty, zz, kx, z, ky, second=0)
            landed(ACROSS_Y, ty, zz, ky)
            send(HALF_X, ty, zz, ky, z, kx, second=1)
            send(PARTNER + 1, ty, zz, kx, z, kp)
            send(PARTNER + 2, ty, zz, ky, z, kp)

        both(d, body)

    def diagonal(ty, d):
        def body(zz, below):
            landed(HALF_Y, ty, zz, kd, 0)
            landed(HALF_X, ty, zz, kd, 1)
            send(PARTNER + 3, ty, zz, kd, z, kp)

        both(d, body)

    def known(c):
        remote(vsg.at[0, kk[c]], vsg.at[0, kk[c]], vss.at[c], vsr.at[c], z, kp).wait_recv()

    def partner(ty, j, cols=range(4)):
        for i in cols:
            landed(PARTNER + i, ty, near[j], kk[2 * i + 1])

    def factors(c):
        go(lambda: remote(vsbuf.at[kk[c]], vsg.at[0, k], vss.at[c], vsr.at[c], z, kk[c]))
        go(lambda: remote(vt_in, vtg.at[k], vts.at[c], vtr.at[c], z, kk[c]))

    local[3].wait()
    launch_z(C)
    launch_xy(C)
    low = lax.broadcasted_iota(jnp.int32, (half_w, LANES), 1) < nc
    local[0].wait()
    order = one_hot((nv * half_w, nv * half_w), lambda r, c: c == lax.rem(r, half_w) * nv + r // half_w)
    for s in range(nsl):
        raw = trv[s].astype(f32)
        tall = jnp.concatenate([raw[:, i * LANES:(i + 1) * LANES] for i in range(half_w)], axis=0).astype(bf16)
        tall = dot(order, tall)
        for pair in range(nv // 2):
            even = tall[2 * pair * half_w:(2 * pair + 1) * half_w]
            odd = tall[(2 * pair + 1) * half_w:(2 * pair + 2) * half_w]
            first = jnp.where(low, even, pltpu.roll(odd, nc, 1))
            second = jnp.where(low, pltpu.roll(even, nc, 1), odd)
            at = (pair * nsl + s) * bands
            xb[me, at:at + bands, :] = jnp.concatenate([first, second], axis=0).astype(bf16)
    launch_z(X)
    launch_xy(X)
    local[1].wait()
    shuffle = one_hot(
        (nsl * bands, nsl * bands),
        lambda r, c: c == (r // bands) * bands + 2 * lax.rem(r, half_w) + lax.rem(r // half_w, 2),
    )
    eye = one_hot((depth, depth), lambda r, c: r == c)
    vsx = dot_t(eye, dot(shuffle, vsv[...].reshape(nsl * bands, depth)).astype(bf16)).astype(bf16)
    vsbuf = vsg.at[1]
    vsbuf[...] = vsx.reshape(ns, rows, nsl * bands)
    for c in (1, 2, 4):
        factors(c)
    keep = pltpu.make_async_copy(vsbuf.at[k], vsg.at[0, k], ls.at[7])
    keep.start()


    def widen(t, carry):
        for c in range(ns):
            for s in range(nsl):
                w = slab[table[t, kk[c] * nsl + s]]
                for q in range(nz):
                    wbuf[q, t, c * nsl + s] = w[:, q * LANES:(q + 1) * LANES]
        return carry

    picked = (
        lax.broadcasted_iota(jnp.int32, (nsl * rows, nsl * bands), 0) // rows
        == lax.broadcasted_iota(jnp.int32, (nsl * rows, nsl * bands), 1) // bands
    )

    def fold(places, cols):
        for zz, c in [(near[j], c) for j in places for c in cols]:
            left = jnp.concatenate([vsg[0, kk[c]].astype(f32)] * nsl, axis=0)
            left = jnp.where(picked, left, 0.0).astype(bf16)
            high = nsl * bands
            right = jnp.concatenate([xb[zz * ns + kk[c], i * high:(i + 1) * high] for i in range(nv // 2)], axis=1)
            folded = dot(left, right)
            for s in range(nsl):
                piece = []
                for n in range(nv):
                    wide = folded[s * rows:(s + 1) * rows, (n // 2) * LANES:(n // 2 + 1) * LANES]
                    wide = wide if n % 2 == 0 else pltpu.roll(wide, nc, 1)
                    piece.append(wide[:, :nc])
                fbuf[zz, c * nsl + s] = jnp.concatenate(piece, axis=0).astype(bf16)

    group_word = sum(g * 4 ** i for i, g in enumerate((0, 1, 0, 1, 2, 2, 3, 3)))
    pair_word = sum(p * 2 ** i for i, p in enumerate((0, 0, 1, 1, 0, 1, 0, 1)))

    def shifted(word, by, size):
        return lax.rem(lax.shift_right_logical(word, by), size)

    def unit(i, cols, add):
        g = shifted(near_word, 2 * shifted(jnp.int32(group_word), 2 * i, 4), 4)
        pair = shifted(jnp.int32(pair_word), i, 2)
        qs = [shifted(near_word, 4 * pair, 4), shifted(near_word, 4 * pair + 2, 4)]
        for c in cols:
            for s in range(nsl):
                right = jnp.concatenate([cb[q * ns + kk[c], s * nc:(s + 1) * nc] for q in qs], axis=1)
                full = dot(fbuf[g, c * nsl + s], right).astype(bf16)
                for h in range(2):
                    mbuf[h, c * nsl + s] = full[:, h * LANES:(h + 1) * LANES].reshape(nv, rows, LANES)
        for h, t0 in [(h, t0) for h in range(2) for t0 in range(0, tgt, 2)]:
            total = {}
            if add:
                total = {(t, n): abuf[t0 + t, g, qs[h], n] for t in range(2) for n in range(nv)}
            for c in cols:
                m = [[mbuf[h, c * nsl + s, n] for n in range(nv)] for s in range(nsl)]
                for t in range(2):
                    w = [wbuf[qs[h], t0 + t, c * nsl + s] for s in range(nsl)]
                    for n in range(nv):
                        four = (w[0] * m[0][n] + w[1] * m[1][n]) + (w[2] * m[2][n] + w[3] * m[3][n])
                        total[t, n] = total[t, n] + four if (t, n) in total else four
            for t in range(2):
                for n in range(nv):
                    abuf[t0 + t, g, qs[h], n] = total[t, n]

    NEAR, DIAG = (0, 1, 2, 3, 4, 5), (6, 7)

    def units(lo, hi, cols):
        def one(i, carry):
            unit(i, cols, cols is DIAG)
            return carry

        lax.fori_loop(lo, hi, one, 0)

    lowc = lax.broadcasted_iota(jnp.int32, (nv * rows, LANES), 1) < nc
    chunk = nv * rows // 2

    def deal(zz, col):
        src = sent.at[zz, col // 2, pl.ds(pl.multiple_of(lax.rem(col, 2) * chunk, chunk), chunk)]
        return remote(src, got.at[me], fs.at[zz, col], fr.at[z, k], zz, col)

    mine = pltpu.make_async_copy(
        sent.at[z, k // 2, pl.ds(pl.multiple_of(core * chunk, chunk), chunk)], got.at[me], ls.at[8]
    )

    def emit(j):
        g = near[j]

        for i in range(nz):
            zz = lax.rem(z + i + 1, nz)
            right = jnp.concatenate([cb[zz * ns + b, nsl * nc:] for b in range(ns)], axis=0)
            left = jnp.concatenate(
                [
                    jnp.concatenate([abuf[zz * nt + t, g, q].reshape(nv * rows, LANES) for q in range(nz)], axis=1)
                    for t in range(nt)
                ],
                axis=0,
            )
            full = dot(left, right)
            sent[zz, g] = jnp.where(lowc, full[:nv * rows], full[nv * rows:]).astype(bf16)
        for i in range(nz):
            zz = lax.rem(z + i + 1, nz)
            for h in range(2):
                if i < nz - 1:
                    deal(zz, 2 * g + h).start()
                else:
                    self = 2 * g + h == k
                    pl.when(jnp.logical_not(self))(lambda: deal(zz, 2 * g + h).start())
                    pl.when(self)(lambda: mine.start())

    own(C, 1)
    side_columns(C, 0)
    for c in (3, 5, 6):
        factors(c)
    own(X, 1)
    side_columns(X, 0)
    local[5].wait()
    local[6].wait()
    lax.fori_loop(0, tgt, widen, 0)
    own(C, 2)
    side_columns(C, 1)
    own(X, 2)
    side_columns(X, 1)
    own(C, 3)
    diagonal(C, 0)
    own(X, 3)
    known(6)
    factors(7)
    keep.wait()
    side_columns(C, 2)
    diagonal(X, 0)
    for c in range(1, 6):
        known(c)
    for j in (0, 1):
        partner(C, j, (0, 1, 2))
        partner(X, j, (0, 1, 2))
    fold((0, 1), NEAR)
    units(0, 2, NEAR)
    side_columns(C, 3)
    side_columns(X, 2)
    diagonal(C, 1)
    partner(C, 2, (0, 1, 2))
    partner(C, 3, (0, 1, 2))
    units(2, 4, NEAR)
    side_columns(X, 3)
    diagonal(X, 1)
    diagonal(C, 2)
    diagonal(C, 3)
    known(7)
    for j in (0, 1):
        partner(C, j, (3,))
        partner(X, j, (3,))
    fold((0, 1), DIAG)
    units(0, 2, DIAG)
    partner(X, 2, (0, 1, 2))
    partner(X, 3, (0, 1, 2))
    fold((2, 3), NEAR)
    units(4, 6, NEAR)
    diagonal(X, 2)
    diagonal(X, 3)
    partner(C, 2, (3,))
    partner(C, 3, (3,))
    units(2, 4, DIAG)
    emit(0)
    emit(1)
    units(6, 8, NEAR)
    partner(X, 2, (3,))
    partner(X, 3, (3,))
    fold((2, 3), DIAG)
    units(4, 6, DIAG)
    emit(2)
    units(6, 8, DIAG)
    emit(3)
    for make, conds in started:
        done = lambda make=make: make().wait_send()
        if conds:
            pl.when(functools.reduce(jnp.logical_and, conds))(done)
        else:
            done()
    local[4].wait()
    for c in range(1, ns):
        remote(vtg.at[kk[c]], vtg.at[kk[c]], vts.at[c], vtr.at[c], z, kp).wait_recv()
    parity = one_hot(
        (nt * bands, nt * bands),
        lambda r, c: c == lax.rem(r // half_w, nt) * bands + 2 * lax.rem(r, half_w) + r // (nt * half_w),
    )
    left = jnp.concatenate([vtg[b].reshape(nt * bands, pk) for b in range(ns)], axis=1)
    left = dot(parity, left).astype(bf16)
    mine.wait()

    def settle(i, carry):
        other = lax.rem(me + i, nz * ns)
        zz, col = other // ns, lax.rem(other, ns)
        deal(zz, col).wait_send()
        remote(got.at[other], got.at[other], fs.at[zz, col], fr.at[zz, col], z, kp).wait_recv()
        return carry

    lax.fori_loop(1, nz * ns, settle, 0)
    for n in range(result.shape[1]):
        right = jnp.concatenate([got[i, n * rows:(n + 1) * rows, :] for i in range(nz * ns)], axis=0)
        full = dot(left, right)
        for t in range(nt):
            even = full[t * half_w:(t + 1) * half_w]
            odd = full[(nt + t) * half_w:(nt + t + 1) * half_w]
            if t == 0:
                odd = pltpu.roll(odd, nc, 1)
            else:
                even = pltpu.roll(even, nc, 1)
            result[t, n] = jnp.where(low, even, odd)


def scoped(nz, ns, shapes, *refs):
    pl.run_scoped(
        lambda *bufs: fused_kernel(*bufs, nz, ns, *refs), *[pltpu.VMEM(shape, jnp.bfloat16) for shape in shapes]
    )


def local(val_target, cond_target, val_source, cond_source, trial_vectors, screened, pair_momentum):
    nz, ns = lax.axis_size("kt"), lax.axis_size("ks")
    nt, bands, pk = val_target.shape
    nc = cond_target.shape[1]
    nsl, _, pz = val_source.shape
    nv = trial_vectors.shape[1]
    rows, width = screened.shape[1:]
    nvec = nv * nz
    nloc = nvec // ns
    bf16, f32 = jnp.bfloat16, jnp.float32
    count, nsrc = nz * ns, ns * nsl
    shapes = [
        (nz, nz * nt, nsrc, rows, LANES),
        (2, nsrc, nv, rows, LANES),
        (nz * nt, nz, nz, nv, rows, LANES),
        (nz, nsrc, nv * rows, nc),
    ]
    dma = pltpu.SemaphoreType.DMA
    out = pl.pallas_call(
        functools.partial(scoped, nz, ns, shapes),
        out_shape=jax.ShapeDtypeStruct((nt, nloc, bands // 2, LANES), f32),
        in_specs=[HBM] * 7,
        out_specs=pl.BlockSpec(memory_space=pltpu.VMEM),
        scratch_shapes=[
            pltpu.VMEM((count, nsl * nc + pk, LANES), bf16),
            pltpu.VMEM((count, nv // 2 * nsl * bands, LANES), bf16),
            pltpu.VMEM((2, ns, rows, nsl * bands), bf16),
            pltpu.VMEM((ns, *val_target.shape), bf16),
            pltpu.VMEM(screened.shape, bf16),
            pltpu.VMEM(trial_vectors.shape, bf16),
            pltpu.VMEM(val_source.shape, bf16),
            pltpu.VMEM(cond_target.shape, bf16),
            pltpu.SMEM(pair_momentum.shape, jnp.int32),
            pltpu.VMEM((nz, nz, nv * rows, nt * nc), bf16),
            pltpu.VMEM((count, nloc * rows, nt * nc), bf16),
            dma((PARTNER + 4, 2, nz)), dma((PARTNER + 4, 2, nz)),
            dma((ns,)), dma((ns,)), dma((ns,)), dma((ns,)), dma((nz, ns)), dma((nz, ns)), dma((9,)),
        ],
        compiler_params=pltpu.CompilerParams(
            collective_id=0, has_side_effects=True, vmem_limit_bytes=67_043_328
        ),
        name="fused",
    )(pair_momentum, screened, val_target, cond_target, val_source, cond_source.reshape(nsl * nc, pz), trial_vectors)
    return out.reshape(nt, nloc, bands * nc)


def fits(mesh, args):
    val_target, cond_target, val_source, cond_source, trial_vectors, screened, pair_momentum = args
    nz, ns = mesh.shape["kt"], mesh.shape["ks"]
    aux = val_target.shape[2]
    nt, nvec, nc = val_target.shape[0] // nz, trial_vectors.shape[1], cond_target.shape[1]
    rows, bands = aux // (nz * ns), val_target.shape[1]
    nsl = val_source.shape[0] // ns
    return (
        ns == 8 and nz == 4 and nt == 2 and 2 * nc == LANES and aux // nz == LANES and rows == 16 and nsl == 4
        and bands == 32 and nvec == 4 * nz and nvec % ns == 0
    )


def solution(mesh):
    in_specs = (
        P("kt", None, "ks"),
        P("kt", None, "ks"),
        P("ks", None, "kt"),
        P("ks", None, "kt"),
        P("ks", "kt", None),
        P(None, ("kt", "ks"), None),
        P(),
    )
    out_specs = P("kt", "ks", None)

    def whole(*args):
        body = local if fits(mesh, args) else general
        return jax.shard_map(body, mesh=mesh, in_specs=in_specs, out_specs=out_specs, check_vma=False)(*args)

    return whole
```

```python
import functools

import jax
import jax.numpy as jnp
from jax import lax
from jax.experimental import pallas as pl
from jax.experimental.pallas import tpu as pltpu
from jax.sharding import PartitionSpec as P


def general(val_target, cond_target, val_source, cond_source, trial_vectors, screened, pair_momentum):
    tgt_val, tgt_cond = (
        lax.all_gather(val_target, "ks", axis=2, tiled=True),
        lax.all_gather(cond_target, "ks", axis=2, tiled=True),
    )
    src_val, src_cond, vectors = (
        lax.all_gather(val_source, "kt", axis=2, tiled=True),
        lax.all_gather(cond_source, "kt", axis=2, tiled=True),
        lax.all_gather(trial_vectors, "kt", axis=1, tiled=True),
    )
    count_kt = lax.axis_size("kt")
    count_ks = lax.axis_size("ks")
    tgt_count = tgt_val.shape[0]
    src_count = src_val.shape[0]
    pair_count = tgt_count * src_count
    width = screened.shape[2]
    val_bands = tgt_val.shape[1]
    cond_bands = tgt_cond.shape[1]
    vec_count = vectors.shape[1]
    table = pair_momentum.reshape(count_kt, tgt_count, count_ks, src_count)
    table = table.transpose(1, 3, 0, 2).reshape(pair_count, count_kt * count_ks)
    outgoing = screened[table]
    arrived = lax.all_to_all(outgoing, ("kt", "ks"), split_axis=1, concat_axis=1, tiled=True)
    pair_mats = arrived.reshape(tgt_count, src_count, width, width)
    trial_four = vectors.reshape(src_count, vec_count, val_bands, cond_bands)
    dressed = jnp.einsum(
        "snwc,scq->snwq", trial_four, src_cond, preferred_element_type=jnp.float32
    ).astype(jnp.bfloat16)
    pair_prod = (
        tgt_val.astype(jnp.float32)[:, None, :, None, :]
        * src_val.astype(jnp.float32)[None, :, None, :, :]
    ).astype(jnp.bfloat16)
    kernels = jnp.einsum(
        "tsvwp,tspq->tsvwq", pair_prod, pair_mats, preferred_element_type=jnp.float32
    ).astype(jnp.bfloat16)
    reduced = jnp.einsum(
        "tsvwq,snwq->tvnq", kernels, dressed, preferred_element_type=jnp.float32
    ).astype(jnp.bfloat16)
    partial_out = jnp.einsum(
        "tvnq,tcq->tnvc", reduced, tgt_cond, preferred_element_type=jnp.float32
    )
    partial_out = partial_out.reshape(tgt_count, vec_count, val_bands * cond_bands)
    return lax.psum_scatter(
        partial_out.astype(jnp.bfloat16), "ks", scatter_dimension=1, tiled=True
    ).astype(jnp.float32)


MESH = pl.DeviceIdType.MESH
HBM = pl.BlockSpec(memory_space=pltpu.MemorySpace.HBM)
C, X = range(2)
UP, DOWN, ACROSS_X, ACROSS_Y, HALF_Y, HALF_X, DIAG_UP, DIAG_DOWN, PARTNER = range(9)
LANES = 128


def remote(src, dst, send, recv, kt, ks):
    return pltpu.make_async_remote_copy(
        src_ref=src, dst_ref=dst, send_sem=send, recv_sem=recv, device_id=(kt, ks), device_id_type=MESH
    )


def nearest(nz):
    packed = []
    for place in range(nz):
        word = 0
        for own in range(nz):
            ranked = sorted(range(nz), key=lambda other: (abs(other - own), other))
            word |= ranked[place] << (2 * own)
        packed.append(word)
    return packed


def one_hot(shape, hit):
    row = lax.broadcasted_iota(jnp.int32, shape, 0)
    col = lax.broadcasted_iota(jnp.int32, shape, 1)
    return jnp.where(hit(row, col), 1.0, 0.0).astype(jnp.bfloat16)


def dot(a, b):
    return jnp.dot(a, b, preferred_element_type=jnp.float32)


def dot_t(a, b):
    return lax.dot_general(a, b, (((1,), (1,)), ((), ())), preferred_element_type=jnp.float32)


def fused_kernel(wbuf, mbuf, nbuf, abuf, fbuf, nz, ns, table_in, screened, vt_in, ct_in, vs_in, cs_in, tr_in, result,
                 cb, xb, vsg, vtg, slab, trv, vsv, ctv, table, sent, got,
                 ss, rs, vss, vsr, vts, vtr, fs, fr, ls):
    bf16, f32 = jnp.bfloat16, jnp.float32
    z, k = lax.axis_index("kt"), lax.axis_index("ks")
    core, side, deep = lax.rem(k, 2), lax.rem(k // 2, 2), k // 4

    def flipped(c):
        return lax.rem(core + c % 2, 2) + 2 * lax.rem(side + (c // 2) % 2, 2) + 4 * lax.rem(deep + c // 4, 2)

    kk = [flipped(c) for c in range(ns)]
    kp, kx, ky, kd = kk[1], kk[2], kk[4], kk[6]
    me = z * ns + k
    z_up, z_down = z + 1, z - 1
    near = [lax.rem(lax.shift_right_logical(jnp.int32(word), 2 * z), 4) for word in nearest(nz)]
    bufs = [cb, xb]
    nsl, bands, depth = vs_in.shape
    nt, _, pk = vt_in.shape
    nc = ct_in.shape[1]
    nv = tr_in.shape[1]
    rows, width = slab.shape[1:]
    nsrc, tgt, nvec = ns * nsl, nz * nt, nz * nv
    half_w = bands // 2
    near_word = sum(near[j] * 4 ** j for j in range(nz))

    local = [
        (tr_in, trv), (vs_in, vsv), (ct_in, ctv), (cs_in, cb.at[me]), (vt_in, vtg.at[k]), (table_in, table), (screened, slab),
    ]
    local = [pltpu.make_async_copy(src, dst, ls.at[i]) for i, (src, dst) in enumerate(local)]
    for copy in local:
        copy.start()

    barrier = pltpu.get_barrier_semaphore()

    def greet(kt, ks):
        pl.semaphore_signal(barrier, inc=1, device_id=(kt, ks), device_id_type=MESH)

    has_up, has_down = z < nz - 1, z > 0
    for peer in (kp, kx, ky):
        greet(z, peer)
    pl.when(has_up)(lambda: greet(z + 1, k))
    pl.when(has_down)(lambda: greet(z - 1, k))

    inner = jnp.logical_and(has_up, has_down)
    pl.when(inner)(lambda: pl.semaphore_wait(barrier, 5))
    pl.when(jnp.logical_not(inner))(lambda: pl.semaphore_wait(barrier, 4))

    started, guard = [], []

    def go(make, when=None):
        conds = guard + ([] if when is None else [when])
        started.append((make, conds))
        if when is None:
            make().start()
        else:
            pl.when(when)(lambda: make().start())

    def under(cond, body):
        guard.append(cond)
        pl.when(cond)(body)
        guard.pop()

    def both(d, body):
        if d == 0:
            body(z, None)
        else:
            for zz, there, below in ((z - d, z >= d, True), (z + d, z + d < nz, False)):
                under(there, functools.partial(body, zz, below))

    def slot(ty, zz, col):
        return bufs[ty].at[zz * ns + col]

    def part(ty, zz, col, second):
        n = bufs[ty].shape[1] // 2
        return slot(ty, zz, col).at[pl.ds(n * second, n)]

    def send(kind, ty, zz, col, kt, ks, when=None, src=None, second=None):
        def make():
            dst = slot(ty, zz, col) if second is None else part(ty, zz, col, second)
            return remote(dst if src is None else src, dst, ss.at[kind, ty, zz], rs.at[kind, ty, zz], kt, ks)

        go(make, when)

    def landed(kind, ty, zz, col, second=None):
        dst = slot(ty, zz, col) if second is None else part(ty, zz, col, second)
        remote(dst, dst, ss.at[kind, ty, zz], rs.at[kind, ty, zz], z, kp).wait_recv()

    def launch_z(ty, src=None):
        send(UP, ty, z, k, z_up, k, has_up, src)
        send(DOWN, ty, z, k, z_down, k, has_down, src)

    def launch_xy(ty):
        send(ACROSS_X, ty, z, k, z, kx)
        send(ACROSS_Y, ty, z, k, z, ky)
        send(PARTNER, ty, z, k, z, kp)

    def own(ty, d):
        def body(zz, below):
            landed(UP if below else DOWN, ty, zz, k)
            if below:
                send(UP, ty, zz, k, z_up, k, has_up)
            else:
                send(DOWN, ty, zz, k, z_down, k, has_down)
            send(ACROSS_X, ty, zz, k, z, kx)
            send(ACROSS_Y, ty, zz, k, z, ky)
            send(PARTNER, ty, zz, k, z, kp)

        both(d, body)

    def side_columns(ty, d):
        def body(zz, below):
            landed(ACROSS_X, ty, zz, kx)
            if d != 1:
                send(HALF_Y, ty, zz, kx, z, ky, second=0)
            landed(ACROSS_Y, ty, zz, ky)
            if d != 1:
                send(HALF_X, ty, zz, ky, z, kx, second=1)
            send(PARTNER + 1, ty, zz, kx, z, kp)
            send(PARTNER + 2, ty, zz, ky, z, kp)

        both(d, body)

    def diagonal(ty, d):
        def body(zz, below):
            if d == 1:
                landed(DIAG_UP if below else DIAG_DOWN, ty, zz, kd)
            else:
                landed(HALF_Y, ty, zz, kd, 0)
                landed(HALF_X, ty, zz, kd, 1)
            if d == 0:
                send(DIAG_UP, ty, zz, kd, z_up, k, has_up)
                send(DIAG_DOWN, ty, zz, kd, z_down, k, has_down)
            send(PARTNER + 3, ty, zz, kd, z, kp)

        both(d, body)

    def known(c):
        remote(vsg.at[0, kk[c]], vsg.at[0, kk[c]], vss.at[c], vsr.at[c], z, kp).wait_recv()

    def partner(ty, j, cols=range(4)):
        for i in cols:
            landed(PARTNER + i, ty, near[j], kk[2 * i + 1])

    def factors(c):
        go(lambda: remote(vsbuf.at[kk[c]], vsg.at[0, k], vss.at[c], vsr.at[c], z, kk[c]))
        go(lambda: remote(vt_in, vtg.at[k], vts.at[c], vtr.at[c], z, kk[c]))

    local[3].wait()
    launch_z(C)
    launch_xy(C)
    low = lax.broadcasted_iota(jnp.int32, (half_w, LANES), 1) < nc
    local[0].wait()
    order = one_hot((nv * half_w, nv * half_w), lambda r, c: c == lax.rem(r, half_w) * nv + r // half_w)
    for s in range(nsl):
        raw = trv[s].astype(f32)
        tall = jnp.concatenate([raw[:, i * LANES:(i + 1) * LANES] for i in range(half_w)], axis=0).astype(bf16)
        tall = dot(order, tall)
        for pair in range(nv // 2):
            even = tall[2 * pair * half_w:(2 * pair + 1) * half_w]
            odd = tall[(2 * pair + 1) * half_w:(2 * pair + 2) * half_w]
            first = jnp.where(low, even, pltpu.roll(odd, nc, 1))
            second = jnp.where(low, pltpu.roll(even, nc, 1), odd)
            at = (pair * nsl + s) * bands
            xb[me, at:at + bands, :] = jnp.concatenate([first, second], axis=0).astype(bf16)
    local[2].wait()
    xb[me, nv // 2 * nsl * bands:] = dot_t(one_hot((pk, pk), lambda r, c: r == c), ctv[...].reshape(nt * nc, pk)).astype(bf16)
    launch_z(X)
    launch_xy(X)
    local[1].wait()
    shuffle = one_hot(
        (nsl * bands, nsl * bands),
        lambda r, c: c == (r // bands) * bands + 2 * lax.rem(r, half_w) + lax.rem(r // half_w, 2),
    )
    eye = one_hot((depth, depth), lambda r, c: r == c)
    vsx = dot_t(eye, dot(shuffle, vsv[...].reshape(nsl * bands, depth)).astype(bf16)).astype(bf16)
    vsbuf = vsg.at[1]
    vsbuf[...] = vsx.reshape(ns, rows, nsl * bands)
    for c in (1, 2, 4):
        factors(c)
    keep = pltpu.make_async_copy(vsbuf.at[k], vsg.at[0, k], ls.at[7])
    keep.start()


    def widen(t, carry):
        for c in range(ns):
            for s in range(nsl):
                w = slab[table[t, kk[c] * nsl + s]]
                for q in range(nz):
                    wbuf[q, t, c * nsl + s] = w[:, q * LANES:(q + 1) * LANES]
        return carry

    picked = (
        lax.broadcasted_iota(jnp.int32, (nsl * rows, nsl * bands), 0) // rows
        == lax.broadcasted_iota(jnp.int32, (nsl * rows, nsl * bands), 1) // bands
    )

    def fold(places, cols):
        for zz, c in [(near[j], c) for j in places for c in cols]:
            left = jnp.concatenate([vsg[0, kk[c]].astype(f32)] * nsl, axis=0)
            left = jnp.where(picked, left, 0.0).astype(bf16)
            high = nsl * bands
            right = jnp.concatenate([xb[zz * ns + kk[c], i * high:(i + 1) * high] for i in range(nv // 2)], axis=1)
            folded = dot(left, right)
            for s in range(nsl):
                piece = []
                for n in range(nv):
                    wide = folded[s * rows:(s + 1) * rows, (n // 2) * LANES:(n // 2 + 1) * LANES]
                    wide = wide if n % 2 == 0 else pltpu.roll(wide, nc, 1)
                    piece.append(wide[:, :nc])
                fbuf[zz, c * nsl + s] = jnp.concatenate(piece, axis=0).astype(bf16)

    group_word = sum(g * 4 ** i for i, g in enumerate((0, 1, 0, 1, 2, 2, 3, 3)))
    pair_word = sum(p * 2 ** i for i, p in enumerate((0, 0, 1, 1, 0, 1, 0, 1)))

    def shifted(word, by, size):
        return lax.rem(lax.shift_right_logical(word, by), size)

    def place(i):
        g = shifted(near_word, 2 * shifted(jnp.int32(group_word), 2 * i, 4), 4)
        pair = shifted(jnp.int32(pair_word), i, 2)
        return g, [shifted(near_word, 4 * pair, 4), shifted(near_word, 4 * pair + 2, 4)]

    def expand(buf, i, cols):
        g, qs = place(i)
        for c in cols:
            for s in range(nsl):
                right = jnp.concatenate([cb[q * ns + kk[c], s * nc:(s + 1) * nc] for q in qs], axis=1)
                full = dot(fbuf[g, c * nsl + s], right).astype(bf16)
                for h in range(2):
                    buf[h, c * nsl + s] = full[:, h * LANES:(h + 1) * LANES].reshape(nv, rows, LANES)

    def contract(buf, i, cols, add):
        g, qs = place(i)
        for h, t0 in [(h, t0) for h in range(2) for t0 in range(0, tgt, 2)]:
            total = {}
            if add:
                total = {(t, n): abuf[t0 + t, g, qs[h], n] for t in range(2) for n in range(nv)}
            for c in cols:
                m = [[buf[h, c * nsl + s, n] for n in range(nv)] for s in range(nsl)]
                for t in range(2):
                    w = [wbuf[qs[h], t0 + t, c * nsl + s] for s in range(nsl)]
                    for n in range(nv):
                        four = (w[0] * m[0][n] + w[1] * m[1][n]) + (w[2] * m[2][n] + w[3] * m[3][n])
                        total[t, n] = total[t, n] + four if (t, n) in total else four
            for t in range(2):
                for n in range(nv):
                    abuf[t0 + t, g, qs[h], n] = total[t, n]

    NEAR, DIAG = (0, 1, 2, 3, 4, 5), (6, 7)

    def units(lo, hi, cols):
        turns = [(buf, i) for buf, i in zip((mbuf, nbuf), range(lo, hi))]
        for buf, i in turns:
            expand(buf, i, cols)
        for buf, i in turns:
            contract(buf, i, cols, cols is DIAG)

    lowc = lax.broadcasted_iota(jnp.int32, (nv * rows, LANES), 1) < nc
    chunk = nv * rows // 2

    def deal(zz, col):
        src = sent.at[zz, col // 2, pl.ds(pl.multiple_of(lax.rem(col, 2) * chunk, chunk), chunk)]
        return remote(src, got.at[me], fs.at[zz, col], fr.at[z, k], zz, col)

    mine = pltpu.make_async_copy(
        sent.at[z, k // 2, pl.ds(pl.multiple_of(core * chunk, chunk), chunk)], got.at[me], ls.at[8]
    )

    def emit(j):
        g = near[j]

        for i in range(nz):
            zz = lax.rem(z + i + 1, nz)
            right = jnp.concatenate([xb[zz * ns + b, nv // 2 * nsl * bands:] for b in range(ns)], axis=0)
            left = jnp.concatenate(
                [
                    jnp.concatenate([abuf[zz * nt + t, g, q].reshape(nv * rows, LANES) for q in range(nz)], axis=1)
                    for t in range(nt)
                ],
                axis=0,
            )
            full = dot(left, right)
            sent[zz, g] = jnp.where(lowc, full[:nv * rows], full[nv * rows:]).astype(bf16)
        for i in range(nz):
            zz = lax.rem(z + i + 1, nz)
            for h in range(2):
                if i < nz - 1:
                    deal(zz, 2 * g + h).start()
                else:
                    self = 2 * g + h == k
                    pl.when(jnp.logical_not(self))(lambda: deal(zz, 2 * g + h).start())
                    pl.when(self)(lambda: mine.start())

    own(C, 1)
    side_columns(C, 0)
    for c in (3, 5, 6):
        factors(c)
    own(X, 1)
    side_columns(X, 0)
    local[5].wait()
    local[6].wait()
    lax.fori_loop(0, tgt, widen, 0)
    own(C, 2)
    side_columns(C, 1)
    diagonal(C, 0)
    own(X, 2)
    own(C, 3)
    side_columns(X, 1)
    known(6)
    factors(7)
    keep.wait()
    for c in range(1, 6):
        known(c)
    for j in (0, 1):
        partner(C, j, (0, 1, 2))
        partner(X, j, (0, 1, 2))
    fold((0, 1), NEAR)
    units(0, 2, NEAR)
    diagonal(X, 0)
    own(X, 3)
    side_columns(C, 2)
    diagonal(C, 1)
    side_columns(C, 3)
    side_columns(X, 2)
    partner(C, 2, (0, 1, 2))
    partner(C, 3, (0, 1, 2))
    units(2, 4, NEAR)
    side_columns(X, 3)
    diagonal(X, 1)
    diagonal(C, 2)
    diagonal(C, 3)
    partner(X, 2, (0, 1, 2))
    partner(X, 3, (0, 1, 2))
    fold((2, 3), NEAR)
    units(4, 6, NEAR)
    diagonal(X, 2)
    diagonal(X, 3)
    known(7)
    for j in (0, 1):
        partner(C, j, (3,))
        partner(X, j, (3,))
    fold((0, 1), DIAG)
    units(0, 2, DIAG)
    partner(C, 2, (3,))
    partner(C, 3, (3,))
    units(2, 4, DIAG)
    units(6, 8, NEAR)
    partner(X, 2, (3,))
    partner(X, 3, (3,))
    emit(0)
    emit(1)
    fold((2, 3), DIAG)
    units(4, 6, DIAG)
    emit(2)
    units(6, 8, DIAG)
    emit(3)
    for make, conds in started:
        done = lambda make=make: make().wait_send()
        if conds:
            pl.when(functools.reduce(jnp.logical_and, conds))(done)
        else:
            done()
    local[4].wait()
    for c in range(1, ns):
        remote(vtg.at[kk[c]], vtg.at[kk[c]], vts.at[c], vtr.at[c], z, kp).wait_recv()
    parity = one_hot(
        (nt * bands, nt * bands),
        lambda r, c: c == lax.rem(r // half_w, nt) * bands + 2 * lax.rem(r, half_w) + r // (nt * half_w),
    )
    left = jnp.concatenate([vtg[b].reshape(nt * bands, pk) for b in range(ns)], axis=1)
    left = dot(parity, left).astype(bf16)
    mine.wait()

    def settle(i, carry):
        other = lax.rem(me + i, nz * ns)
        zz, col = other // ns, lax.rem(other, ns)
        deal(zz, col).wait_send()
        remote(got.at[other], got.at[other], fs.at[zz, col], fr.at[zz, col], z, kp).wait_recv()
        return carry

    lax.fori_loop(1, nz * ns, settle, 0)
    for n in range(result.shape[1]):
        right = jnp.concatenate([got[i, n * rows:(n + 1) * rows, :] for i in range(nz * ns)], axis=0)
        full = dot(left, right)
        for t in range(nt):
            even = full[t * half_w:(t + 1) * half_w]
            odd = full[(nt + t) * half_w:(nt + t + 1) * half_w]
            if t == 0:
                odd = pltpu.roll(odd, nc, 1)
            else:
                even = pltpu.roll(even, nc, 1)
            result[t, n] = jnp.where(low, even, odd)


def scoped(nz, ns, shapes, *refs):
    pl.run_scoped(
        lambda *bufs: fused_kernel(*bufs, nz, ns, *refs), *[pltpu.VMEM(shape, jnp.bfloat16) for shape in shapes]
    )


def local(val_target, cond_target, val_source, cond_source, trial_vectors, screened, pair_momentum):
    nz, ns = lax.axis_size("kt"), lax.axis_size("ks")
    nt, bands, pk = val_target.shape
    nc = cond_target.shape[1]
    nsl, _, pz = val_source.shape
    nv = trial_vectors.shape[1]
    rows, width = screened.shape[1:]
    nvec = nv * nz
    nloc = nvec // ns
    bf16, f32 = jnp.bfloat16, jnp.float32
    count, nsrc = nz * ns, ns * nsl
    shapes = [
        (nz, nz * nt, nsrc, rows, LANES),
        (2, nsrc, nv, rows, LANES),
        (2, nsrc, nv, rows, LANES),
        (nz * nt, nz, nz, nv, rows, LANES),
        (nz, nsrc, nv * rows, nc),
    ]
    dma = pltpu.SemaphoreType.DMA
    out = pl.pallas_call(
        functools.partial(scoped, nz, ns, shapes),
        out_shape=jax.ShapeDtypeStruct((nt, nloc, bands // 2, LANES), f32),
        in_specs=[HBM] * 7,
        out_specs=pl.BlockSpec(memory_space=pltpu.VMEM),
        scratch_shapes=[
            pltpu.VMEM((count, nsl * nc, LANES), bf16),
            pltpu.VMEM((count, nv // 2 * nsl * bands + pk, LANES), bf16),
            pltpu.VMEM((2, ns, rows, nsl * bands), bf16),
            pltpu.VMEM((ns, *val_target.shape), bf16),
            pltpu.VMEM(screened.shape, bf16),
            pltpu.VMEM(trial_vectors.shape, bf16),
            pltpu.VMEM(val_source.shape, bf16),
            pltpu.VMEM(cond_target.shape, bf16),
            pltpu.SMEM(pair_momentum.shape, jnp.int32),
            pltpu.VMEM((nz, nz, nv * rows, nt * nc), bf16),
            pltpu.VMEM((count, nloc * rows, nt * nc), bf16),
            dma((PARTNER + 4, 2, nz)), dma((PARTNER + 4, 2, nz)),
            dma((ns,)), dma((ns,)), dma((ns,)), dma((ns,)), dma((nz, ns)), dma((nz, ns)), dma((9,)),
        ],
        compiler_params=pltpu.CompilerParams(
            collective_id=0, has_side_effects=True, vmem_limit_bytes=67_043_328
        ),
        name="fused",
    )(pair_momentum, screened, val_target, cond_target, val_source, cond_source.reshape(nsl * nc, pz), trial_vectors)
    return out.reshape(nt, nloc, bands * nc)


def fits(mesh, args):
    val_target, cond_target, val_source, cond_source, trial_vectors, screened, pair_momentum = args
    nz, ns = mesh.shape["kt"], mesh.shape["ks"]
    aux = val_target.shape[2]
    nt, nvec, nc = val_target.shape[0] // nz, trial_vectors.shape[1], cond_target.shape[1]
    rows, bands = aux // (nz * ns), val_target.shape[1]
    nsl = val_source.shape[0] // ns
    return (
        ns == 8 and nz == 4 and nt == 2 and 2 * nc == LANES and aux // nz == LANES and rows == 16 and nsl == 4
        and bands == 32 and nvec == 4 * nz and nvec % ns == 0
    )


def solution(mesh):
    in_specs = (
        P("kt", None, "ks"),
        P("kt", None, "ks"),
        P("ks", None, "kt"),
        P("ks", None, "kt"),
        P("ks", "kt", None),
        P(None, ("kt", "ks"), None),
        P(),
    )
    out_specs = P("kt", "ks", None)

    def whole(*args):
        body = local if fits(mesh, args) else general
        return jax.shard_map(body, mesh=mesh, in_specs=in_specs, out_specs=out_specs, check_vma=False)(*args)

    return whole
```

```python
import functools

import jax
import jax.numpy as jnp
from jax import lax
from jax.experimental import pallas as pl
from jax.experimental.pallas import tpu as pltpu
from jax.sharding import PartitionSpec as P


def general(val_target, cond_target, val_source, cond_source, trial_vectors, screened, pair_momentum):
    tgt_val, tgt_cond = (
        lax.all_gather(val_target, "ks", axis=2, tiled=True),
        lax.all_gather(cond_target, "ks", axis=2, tiled=True),
    )
    src_val, src_cond, vectors = (
        lax.all_gather(val_source, "kt", axis=2, tiled=True),
        lax.all_gather(cond_source, "kt", axis=2, tiled=True),
        lax.all_gather(trial_vectors, "kt", axis=1, tiled=True),
    )
    count_kt = lax.axis_size("kt")
    count_ks = lax.axis_size("ks")
    tgt_count = tgt_val.shape[0]
    src_count = src_val.shape[0]
    pair_count = tgt_count * src_count
    width = screened.shape[2]
    val_bands = tgt_val.shape[1]
    cond_bands = tgt_cond.shape[1]
    vec_count = vectors.shape[1]
    table = pair_momentum.reshape(count_kt, tgt_count, count_ks, src_count)
    table = table.transpose(1, 3, 0, 2).reshape(pair_count, count_kt * count_ks)
    outgoing = screened[table]
    arrived = lax.all_to_all(outgoing, ("kt", "ks"), split_axis=1, concat_axis=1, tiled=True)
    pair_mats = arrived.reshape(tgt_count, src_count, width, width)
    trial_four = vectors.reshape(src_count, vec_count, val_bands, cond_bands)
    dressed = jnp.einsum(
        "snwc,scq->snwq", trial_four, src_cond, preferred_element_type=jnp.float32
    ).astype(jnp.bfloat16)
    pair_prod = (
        tgt_val.astype(jnp.float32)[:, None, :, None, :]
        * src_val.astype(jnp.float32)[None, :, None, :, :]
    ).astype(jnp.bfloat16)
    kernels = jnp.einsum(
        "tsvwp,tspq->tsvwq", pair_prod, pair_mats, preferred_element_type=jnp.float32
    ).astype(jnp.bfloat16)
    reduced = jnp.einsum(
        "tsvwq,snwq->tvnq", kernels, dressed, preferred_element_type=jnp.float32
    ).astype(jnp.bfloat16)
    partial_out = jnp.einsum(
        "tvnq,tcq->tnvc", reduced, tgt_cond, preferred_element_type=jnp.float32
    )
    partial_out = partial_out.reshape(tgt_count, vec_count, val_bands * cond_bands)
    return lax.psum_scatter(
        partial_out.astype(jnp.bfloat16), "ks", scatter_dimension=1, tiled=True
    ).astype(jnp.float32)


MESH = pl.DeviceIdType.MESH
HBM = pl.BlockSpec(memory_space=pltpu.MemorySpace.HBM)
C, X = range(2)
UP, DOWN, ACROSS_X, ACROSS_Y, HALF_Y, HALF_X, DIAG_UP, DIAG_DOWN, PARTNER = range(9)
LANES = 128


def remote(src, dst, send, recv, kt, ks):
    return pltpu.make_async_remote_copy(
        src_ref=src, dst_ref=dst, send_sem=send, recv_sem=recv, device_id=(kt, ks), device_id_type=MESH
    )


def nearest(nz):
    packed = []
    for place in range(nz):
        word = 0
        for own in range(nz):
            ranked = sorted(range(nz), key=lambda other: (abs(other - own), other))
            word |= ranked[place] << (2 * own)
        packed.append(word)
    return packed


def one_hot(shape, hit):
    row = lax.broadcasted_iota(jnp.int32, shape, 0)
    col = lax.broadcasted_iota(jnp.int32, shape, 1)
    return jnp.where(hit(row, col), 1.0, 0.0).astype(jnp.bfloat16)


def dot(a, b):
    return jnp.dot(a, b, preferred_element_type=jnp.float32)


def dot_t(a, b):
    return lax.dot_general(a, b, (((1,), (1,)), ((), ())), preferred_element_type=jnp.float32)


def fused_kernel(wbuf, mbuf, nbuf, abuf, fbuf, nz, ns, table_in, screened, vt_in, ct_in, vs_in, cs_in, tr_in, result,
                 cb, xb, vsg, vtg, slab, trv, vsv, ctv, table, sent, got,
                 ss, rs, vss, vsr, vts, vtr, fs, fr, ls):
    bf16, f32 = jnp.bfloat16, jnp.float32
    z, k = lax.axis_index("kt"), lax.axis_index("ks")
    core, side, deep = lax.rem(k, 2), lax.rem(k // 2, 2), k // 4

    def flipped(c):
        return lax.rem(core + c % 2, 2) + 2 * lax.rem(side + (c // 2) % 2, 2) + 4 * lax.rem(deep + c // 4, 2)

    kk = [flipped(c) for c in range(ns)]
    kp, kx, ky, kd = kk[1], kk[2], kk[4], kk[6]
    me = z * ns + k
    z_up, z_down = z + 1, z - 1
    near = [lax.rem(lax.shift_right_logical(jnp.int32(word), 2 * z), 4) for word in nearest(nz)]
    bufs = [cb, xb]
    nsl, bands, depth = vs_in.shape
    nt, _, pk = vt_in.shape
    nc = ct_in.shape[1]
    nv = tr_in.shape[1]
    rows, width = slab.shape[1:]
    nsrc, tgt, nvec = ns * nsl, nz * nt, nz * nv
    half_w = bands // 2
    near_word = sum(near[j] * 4 ** j for j in range(nz))

    local = [
        (tr_in, trv), (vs_in, vsv), (ct_in, ctv), (cs_in, cb.at[me]), (vt_in, vtg.at[k]), (table_in, table), (screened, slab),
    ]
    local = [pltpu.make_async_copy(src, dst, ls.at[i]) for i, (src, dst) in enumerate(local)]
    for copy in local:
        copy.start()

    barrier = pltpu.get_barrier_semaphore()

    def greet(kt, ks):
        pl.semaphore_signal(barrier, inc=1, device_id=(kt, ks), device_id_type=MESH)

    has_up, has_down = z < nz - 1, z > 0
    for peer in (kp, kx, ky):
        greet(z, peer)
    pl.when(has_up)(lambda: greet(z + 1, k))
    pl.when(has_down)(lambda: greet(z - 1, k))

    inner = jnp.logical_and(has_up, has_down)
    pl.when(inner)(lambda: pl.semaphore_wait(barrier, 5))
    pl.when(jnp.logical_not(inner))(lambda: pl.semaphore_wait(barrier, 4))

    started, guard = [], []

    def go(make, when=None):
        conds = guard + ([] if when is None else [when])
        started.append((make, conds))
        if when is None:
            make().start()
        else:
            pl.when(when)(lambda: make().start())

    def under(cond, body):
        guard.append(cond)
        pl.when(cond)(body)
        guard.pop()

    def both(d, body):
        if d == 0:
            body(z, None)
        else:
            for zz, there, below in ((z - d, z >= d, True), (z + d, z + d < nz, False)):
                under(there, functools.partial(body, zz, below))

    def slot(ty, zz, col):
        return bufs[ty].at[zz * ns + col]

    def part(ty, zz, col, second):
        n = bufs[ty].shape[1] // 2
        return slot(ty, zz, col).at[pl.ds(n * second, n)]

    def send(kind, ty, zz, col, kt, ks, when=None, src=None, second=None):
        def make():
            dst = slot(ty, zz, col) if second is None else part(ty, zz, col, second)
            return remote(dst if src is None else src, dst, ss.at[kind, ty, zz], rs.at[kind, ty, zz], kt, ks)

        go(make, when)

    def landed(kind, ty, zz, col, second=None):
        dst = slot(ty, zz, col) if second is None else part(ty, zz, col, second)
        remote(dst, dst, ss.at[kind, ty, zz], rs.at[kind, ty, zz], z, kp).wait_recv()

    def launch_z(ty, src=None):
        send(UP, ty, z, k, z_up, k, has_up, src)
        send(DOWN, ty, z, k, z_down, k, has_down, src)

    def launch_xy(ty):
        send(ACROSS_X, ty, z, k, z, kx)
        send(ACROSS_Y, ty, z, k, z, ky)
        send(PARTNER, ty, z, k, z, kp)

    def own(ty, d):
        def body(zz, below):
            landed(UP if below else DOWN, ty, zz, k)
            if below:
                send(UP, ty, zz, k, z_up, k, has_up)
            else:
                send(DOWN, ty, zz, k, z_down, k, has_down)
            send(ACROSS_X, ty, zz, k, z, kx)
            send(ACROSS_Y, ty, zz, k, z, ky)
            send(PARTNER, ty, zz, k, z, kp)

        both(d, body)

    def side_columns(ty, d):
        def body(zz, below):
            landed(ACROSS_X, ty, zz, kx)
            if d != 1:
                send(HALF_Y, ty, zz, kx, z, ky, second=0)
            landed(ACROSS_Y, ty, zz, ky)
            if d != 1:
                send(HALF_X, ty, zz, ky, z, kx, second=1)
            send(PARTNER + 1, ty, zz, kx, z, kp)
            send(PARTNER + 2, ty, zz, ky, z, kp)

        both(d, body)

    def diagonal(ty, d):
        def body(zz, below):
            if d == 1:
                landed(DIAG_UP if below else DIAG_DOWN, ty, zz, kd)
            else:
                landed(HALF_Y, ty, zz, kd, 0)
                landed(HALF_X, ty, zz, kd, 1)
            if d == 0:
                send(DIAG_UP, ty, zz, kd, z_up, k, has_up)
                send(DIAG_DOWN, ty, zz, kd, z_down, k, has_down)
            send(PARTNER + 3, ty, zz, kd, z, kp)

        both(d, body)

    def known(c):
        remote(vsg.at[0, kk[c]], vsg.at[0, kk[c]], vss.at[c], vsr.at[c], z, kp).wait_recv()

    def partner(ty, j, cols=range(4)):
        for i in cols:
            landed(PARTNER + i, ty, near[j], kk[2 * i + 1])

    def factors(c):
        go(lambda: remote(vsbuf.at[kk[c]], vsg.at[0, k], vss.at[c], vsr.at[c], z, kk[c]))
        go(lambda: remote(vt_in, vtg.at[k], vts.at[c], vtr.at[c], z, kk[c]))

    local[3].wait()
    launch_z(C)
    launch_xy(C)
    low = lax.broadcasted_iota(jnp.int32, (half_w, LANES), 1) < nc
    local[0].wait()
    order = one_hot((nv * half_w, nv * half_w), lambda r, c: c == lax.rem(r, half_w) * nv + r // half_w)
    for s in range(nsl):
        raw = trv[s].astype(f32)
        tall = jnp.concatenate([raw[:, i * LANES:(i + 1) * LANES] for i in range(half_w)], axis=0).astype(bf16)
        tall = dot(order, tall)
        for pair in range(nv // 2):
            even = tall[2 * pair * half_w:(2 * pair + 1) * half_w]
            odd = tall[(2 * pair + 1) * half_w:(2 * pair + 2) * half_w]
            first = jnp.where(low, even, pltpu.roll(odd, nc, 1))
            second = jnp.where(low, pltpu.roll(even, nc, 1), odd)
            at = (pair * nsl + s) * bands
            xb[me, at:at + bands, :] = jnp.concatenate([first, second], axis=0).astype(bf16)
    local[2].wait()
    xb[me, nv // 2 * nsl * bands:] = dot_t(one_hot((pk, pk), lambda r, c: r == c), ctv[...].reshape(nt * nc, pk)).astype(bf16)
    launch_z(X)
    launch_xy(X)
    local[1].wait()
    shuffle = one_hot(
        (nsl * bands, nsl * bands),
        lambda r, c: c == (r // bands) * bands + 2 * lax.rem(r, half_w) + lax.rem(r // half_w, 2),
    )
    eye = one_hot((depth, depth), lambda r, c: r == c)
    vsx = dot_t(eye, dot(shuffle, vsv[...].reshape(nsl * bands, depth)).astype(bf16)).astype(bf16)
    vsbuf = vsg.at[1]
    vsbuf[...] = vsx.reshape(ns, rows, nsl * bands)
    for c in (1, 2, 4):
        factors(c)
    keep = pltpu.make_async_copy(vsbuf.at[k], vsg.at[0, k], ls.at[7])
    keep.start()


    def widen(t, carry):
        for c in range(ns):
            for s in range(nsl):
                w = slab[table[t, kk[c] * nsl + s]]
                for q in range(nz):
                    wbuf[q, t, c * nsl + s] = w[:, q * LANES:(q + 1) * LANES]
        return carry

    picked = (
        lax.broadcasted_iota(jnp.int32, (nsl * rows, nsl * bands), 0) // rows
        == lax.broadcasted_iota(jnp.int32, (nsl * rows, nsl * bands), 1) // bands
    )

    def fold(places, cols):
        for zz, c in [(near[j], c) for j in places for c in cols]:
            left = jnp.concatenate([vsg[0, kk[c]].astype(f32)] * nsl, axis=0)
            left = jnp.where(picked, left, 0.0).astype(bf16)
            high = nsl * bands
            right = jnp.concatenate([xb[zz * ns + kk[c], i * high:(i + 1) * high] for i in range(nv // 2)], axis=1)
            folded = dot(left, right)
            for s in range(nsl):
                piece = []
                for n in range(nv):
                    wide = folded[s * rows:(s + 1) * rows, (n // 2) * LANES:(n // 2 + 1) * LANES]
                    wide = wide if n % 2 == 0 else pltpu.roll(wide, nc, 1)
                    piece.append(wide[:, :nc])
                fbuf[zz, c * nsl + s] = jnp.concatenate(piece, axis=0).astype(bf16)

    group_word = sum(g * 4 ** i for i, g in enumerate((0, 1, 0, 1, 2, 2, 3, 3)))
    pair_word = sum(p * 2 ** i for i, p in enumerate((0, 0, 1, 1, 0, 1, 0, 1)))

    def shifted(word, by, size):
        return lax.rem(lax.shift_right_logical(word, by), size)

    def place(i):
        g = shifted(near_word, 2 * shifted(jnp.int32(group_word), 2 * i, 4), 4)
        pair = shifted(jnp.int32(pair_word), i, 2)
        return g, [shifted(near_word, 4 * pair, 4), shifted(near_word, 4 * pair + 2, 4)]

    def expand(buf, i, cols):
        g, qs = place(i)
        for c in cols:
            for s in range(nsl):
                right = jnp.concatenate([cb[q * ns + kk[c], s * nc:(s + 1) * nc] for q in qs], axis=1)
                full = dot(fbuf[g, c * nsl + s], right).astype(bf16)
                for h in range(2):
                    buf[h, c * nsl + s] = full[:, h * LANES:(h + 1) * LANES].reshape(nv, rows, LANES)

    def contract(buf, i, cols, add):
        g, qs = place(i)
        for h, t0 in [(h, t0) for h in range(2) for t0 in range(0, tgt, 2)]:
            total = {}
            if add:
                total = {(t, n): abuf[t0 + t, g, qs[h], n] for t in range(2) for n in range(nv)}
            for c in cols:
                m = [[buf[h, c * nsl + s, n] for n in range(nv)] for s in range(nsl)]
                for t in range(2):
                    w = [wbuf[qs[h], t0 + t, c * nsl + s] for s in range(nsl)]
                    for n in range(nv):
                        four = (w[0] * m[0][n] + w[1] * m[1][n]) + (w[2] * m[2][n] + w[3] * m[3][n])
                        total[t, n] = total[t, n] + four if (t, n) in total else four
            for t in range(2):
                for n in range(nv):
                    abuf[t0 + t, g, qs[h], n] = total[t, n]

    OWN, SIDE, NEAR, DIAG = (0, 1), (2, 3, 4, 5), (0, 1, 2, 3, 4, 5), (6, 7)

    def units(lo, hi, cols):
        turns = [(buf, i) for buf, i in zip((mbuf, nbuf), range(lo, hi))]
        for buf, i in turns:
            expand(buf, i, cols)
        for buf, i in turns:
            contract(buf, i, cols, cols in (SIDE, DIAG))

    lowc = lax.broadcasted_iota(jnp.int32, (nv * rows, LANES), 1) < nc
    chunk = nv * rows // 2

    def deal(zz, col):
        src = sent.at[zz, col // 2, pl.ds(pl.multiple_of(lax.rem(col, 2) * chunk, chunk), chunk)]
        return remote(src, got.at[me], fs.at[zz, col], fr.at[z, k], zz, col)

    mine = pltpu.make_async_copy(
        sent.at[z, k // 2, pl.ds(pl.multiple_of(core * chunk, chunk), chunk)], got.at[me], ls.at[8]
    )

    def emit(j):
        g = near[j]

        for i in range(nz):
            zz = lax.rem(z + i + 1, nz)
            right = jnp.concatenate([xb[zz * ns + b, nv // 2 * nsl * bands:] for b in range(ns)], axis=0)
            left = jnp.concatenate(
                [
                    jnp.concatenate([abuf[zz * nt + t, g, q].reshape(nv * rows, LANES) for q in range(nz)], axis=1)
                    for t in range(nt)
                ],
                axis=0,
            )
            full = dot(left, right)
            sent[zz, g] = jnp.where(lowc, full[:nv * rows], full[nv * rows:]).astype(bf16)
        for i in (nz // 2 - 1, *range(nz // 2 - 1), *range(nz // 2, nz)):
            zz = lax.rem(z + i + 1, nz)
            for h in range(2):
                if i < nz - 1:
                    deal(zz, 2 * g + h).start()
                else:
                    self = 2 * g + h == k
                    pl.when(jnp.logical_not(self))(lambda: deal(zz, 2 * g + h).start())
                    pl.when(self)(lambda: mine.start())

    local[5].wait()
    local[6].wait()
    lax.fori_loop(0, tgt, widen, 0)
    own(C, 1)
    side_columns(C, 0)
    for c in (3, 5, 6):
        factors(c)
    own(X, 1)
    side_columns(X, 0)
    own(C, 2)
    side_columns(C, 1)
    diagonal(C, 0)
    own(X, 2)
    own(C, 3)
    side_columns(X, 1)
    known(6)
    factors(7)
    keep.wait()
    for c in range(1, 6):
        known(c)
    for j in (0, 1):
        partner(C, j, (0, 1, 2))
        partner(X, j, (0, 1, 2))
    fold((0, 1), NEAR)
    units(0, 2, NEAR)
    diagonal(X, 0)
    own(X, 3)
    side_columns(C, 2)
    diagonal(C, 1)
    side_columns(C, 3)
    side_columns(X, 2)
    partner(C, 2, (0, 1, 2))
    partner(C, 3, (0, 1, 2))
    units(2, 4, NEAR)
    for j in (2, 3):
        partner(X, j, (0,))
    fold((2, 3), OWN)
    units(4, 6, OWN)
    side_columns(X, 3)
    diagonal(X, 1)
    diagonal(C, 2)
    diagonal(C, 3)
    partner(X, 2, (1, 2))
    partner(X, 3, (1, 2))
    fold((2, 3), SIDE)
    units(4, 6, SIDE)
    diagonal(X, 2)
    diagonal(X, 3)
    known(7)
    for j in (0, 1):
        partner(C, j, (3,))
        partner(X, j, (3,))
    fold((0, 1), DIAG)
    units(0, 2, DIAG)
    partner(C, 2, (3,))
    partner(C, 3, (3,))
    units(2, 4, DIAG)
    units(6, 8, NEAR)
    partner(X, 2, (3,))
    partner(X, 3, (3,))
    emit(0)
    emit(1)
    fold((2, 3), DIAG)
    units(4, 6, DIAG)
    emit(2)
    units(6, 8, DIAG)
    emit(3)
    for make, conds in started:
        done = lambda make=make: make().wait_send()
        if conds:
            pl.when(functools.reduce(jnp.logical_and, conds))(done)
        else:
            done()
    local[4].wait()
    for c in range(1, ns):
        remote(vtg.at[kk[c]], vtg.at[kk[c]], vts.at[c], vtr.at[c], z, kp).wait_recv()
    parity = one_hot(
        (nt * bands, nt * bands),
        lambda r, c: c == lax.rem(r // half_w, nt) * bands + 2 * lax.rem(r, half_w) + r // (nt * half_w),
    )
    left = jnp.concatenate([vtg[b].reshape(nt * bands, pk) for b in range(ns)], axis=1)
    left = dot(parity, left).astype(bf16)
    mine.wait()

    def settle(i, carry):
        other = lax.rem(me + i, nz * ns)
        zz, col = other // ns, lax.rem(other, ns)
        deal(zz, col).wait_send()
        remote(got.at[other], got.at[other], fs.at[zz, col], fr.at[zz, col], z, kp).wait_recv()
        return carry

    lax.fori_loop(1, nz * ns, settle, 0)
    for n in range(result.shape[1]):
        right = jnp.concatenate([got[i, n * rows:(n + 1) * rows, :] for i in range(nz * ns)], axis=0)
        full = dot(left, right)
        for t in range(nt):
            even = full[t * half_w:(t + 1) * half_w]
            odd = full[(nt + t) * half_w:(nt + t + 1) * half_w]
            if t == 0:
                odd = pltpu.roll(odd, nc, 1)
            else:
                even = pltpu.roll(even, nc, 1)
            result[t, n] = jnp.where(low, even, odd)


def scoped(nz, ns, shapes, *refs):
    pl.run_scoped(
        lambda *bufs: fused_kernel(*bufs, nz, ns, *refs), *[pltpu.VMEM(shape, jnp.bfloat16) for shape in shapes]
    )


def local(val_target, cond_target, val_source, cond_source, trial_vectors, screened, pair_momentum):
    nz, ns = lax.axis_size("kt"), lax.axis_size("ks")
    nt, bands, pk = val_target.shape
    nc = cond_target.shape[1]
    nsl, _, pz = val_source.shape
    nv = trial_vectors.shape[1]
    rows, width = screened.shape[1:]
    nvec = nv * nz
    nloc = nvec // ns
    bf16, f32 = jnp.bfloat16, jnp.float32
    count, nsrc = nz * ns, ns * nsl
    shapes = [
        (nz, nz * nt, nsrc, rows, LANES),
        (2, nsrc, nv, rows, LANES),
        (2, nsrc, nv, rows, LANES),
        (nz * nt, nz, nz, nv, rows, LANES),
        (nz, nsrc, nv * rows, nc),
    ]
    dma = pltpu.SemaphoreType.DMA
    out = pl.pallas_call(
        functools.partial(scoped, nz, ns, shapes),
        out_shape=jax.ShapeDtypeStruct((nt, nloc, bands // 2, LANES), f32),
        in_specs=[HBM] * 7,
        out_specs=pl.BlockSpec(memory_space=pltpu.VMEM),
        scratch_shapes=[
            pltpu.VMEM((count, nsl * nc, LANES), bf16),
            pltpu.VMEM((count, nv // 2 * nsl * bands + pk, LANES), bf16),
            pltpu.VMEM((2, ns, rows, nsl * bands), bf16),
            pltpu.VMEM((ns, *val_target.shape), bf16),
            pltpu.VMEM(screened.shape, bf16),
            pltpu.VMEM(trial_vectors.shape, bf16),
            pltpu.VMEM(val_source.shape, bf16),
            pltpu.VMEM(cond_target.shape, bf16),
            pltpu.SMEM(pair_momentum.shape, jnp.int32),
            pltpu.VMEM((nz, nz, nv * rows, nt * nc), bf16),
            pltpu.VMEM((count, nloc * rows, nt * nc), bf16),
            dma((PARTNER + 4, 2, nz)), dma((PARTNER + 4, 2, nz)),
            dma((ns,)), dma((ns,)), dma((ns,)), dma((ns,)), dma((nz, ns)), dma((nz, ns)), dma((9,)),
        ],
        compiler_params=pltpu.CompilerParams(
            collective_id=0, has_side_effects=True, vmem_limit_bytes=67_043_328
        ),
        name="fused",
    )(pair_momentum, screened, val_target, cond_target, val_source, cond_source.reshape(nsl * nc, pz), trial_vectors)
    return out.reshape(nt, nloc, bands * nc)


def fits(mesh, args):
    val_target, cond_target, val_source, cond_source, trial_vectors, screened, pair_momentum = args
    nz, ns = mesh.shape["kt"], mesh.shape["ks"]
    aux = val_target.shape[2]
    nt, nvec, nc = val_target.shape[0] // nz, trial_vectors.shape[1], cond_target.shape[1]
    rows, bands = aux // (nz * ns), val_target.shape[1]
    nsl = val_source.shape[0] // ns
    return (
        ns == 8 and nz == 4 and nt == 2 and 2 * nc == LANES and aux // nz == LANES and rows == 16 and nsl == 4
        and bands == 32 and nvec == 4 * nz and nvec % ns == 0
    )


def solution(mesh):
    in_specs = (
        P("kt", None, "ks"),
        P("kt", None, "ks"),
        P("ks", None, "kt"),
        P("ks", None, "kt"),
        P("ks", "kt", None),
        P(None, ("kt", "ks"), None),
        P(),
    )
    out_specs = P("kt", "ks", None)

    def whole(*args):
        body = local if fits(mesh, args) else general
        return jax.shard_map(body, mesh=mesh, in_specs=in_specs, out_specs=out_specs, check_vma=False)(*args)

    return whole
```
